32 devices in a mesh: gx: 4 (over y, x), gy: 4 (over z), ma: 2 (over core).
Axes of the slice: x: 2, y: 2, z: 4, core: 2. Of those that a mesh axis runs over, the one named last changes fastest.
Arguments:
- object_field: float32 [2, 2048, 1536], P(None, 'gx', 'gy'), may hold values from -6 to 6
- probe: float32 [2, 4, 256, 256], P(None, 'ma'), may hold values from -3 to 3
- offsets: int32 [4, 4, 6, 2], P('gx', 'gy'), may hold values from 0 to 511, as said below
- counts: int32 [4, 4], P('gx', 'gy'), may hold values from 1 to 6, as said below
- amplitude: float32 [4, 4, 6, 256, 256], P('gx', 'gy'), may hold values from 0.5 to 3
Outputs:
- object_grad: float32 [2, 2048, 1536], P(None, ('gx', 'ma'), 'gy')
- probe_grad: float32 [2, 4, 256, 256], P(None, 'ma')
The draws below stay inside these ranges and needn't reach their ends.
Inputs may be any that keep to these rules, and one draw needn't show every extreme that they name: A tile's offsets are below 512 for rows and below 384 for columns; no patch passes the object's last row or column. `counts`: every tile holds at least one live position; in each tile row, tiles v and v + 2 hold at most 8 live positions together; in every draw some tile holds exactly 6 and its partner exactly 2.
All inputs are finite; a program needn't handle non-finite values.
Results may differ from the reference program's by a relative error of at most 0.0003.
Values sent between devices are 32-bit elements; how exact they have to be, the bound alone decides.
A program may use at most 128 MiB of HBM per device.

```python
import jax
import jax.numpy as jnp
from jax import lax

PS = 256
MODES = 4
TR = 512
TC = 384
CAP = 6
BAL = 4
TILES_X = 4
TILES_Y = 4
OX = 2048
OY = 1536


def draw_offsets(key, part):
    keys = jax.random.split(key, 4)
    shape_all = (TILES_X, TILES_Y, CAP)
    tile_row = jnp.arange(TILES_X, dtype=jnp.int32)[:, None, None]
    tile_col = jnp.arange(TILES_Y, dtype=jnp.int32)[None, :, None]
    row_limit = jnp.where(tile_row == TILES_X - 1, TR - PS + 1, TR)
    col_limit = jnp.where(tile_col == TILES_Y - 1, TC - PS + 1, TC)
    row_any = jax.random.randint(keys[0], shape_all, 0, row_limit)
    col_any = jax.random.randint(keys[1], shape_all, 0, col_limit)
    row_near = jax.random.randint(keys[2], shape_all, jnp.maximum(row_limit - PS // 2, 0), row_limit)
    col_near = jax.random.randint(keys[3], shape_all, jnp.maximum(col_limit - PS // 2, 0), col_limit)
    slot_ids = jnp.arange(CAP, dtype=jnp.int32)[None, None, :]
    row_all = jnp.where(slot_ids == 0, row_near, row_any)
    col_all = jnp.where(slot_ids == 0, col_near, col_any)
    row_all = row_all.at[0, 0, 0].set(TR - 1).at[0, 0, 1].set(0)
    col_all = col_all.at[0, 0, 0].set(TC - 1).at[0, 0, 1].set(0)
    return jnp.stack([row_all, col_all], axis=-1).astype(jnp.int32)


def draw_counts(key, part):
    keys = jax.random.split(key, 5)
    half_axis = TILES_Y // 2
    first = jax.random.randint(keys[0], (TILES_X, half_axis), 1, CAP + 1)
    second_limit = jnp.minimum(CAP, 2 * BAL - first)
    second = jax.random.randint(keys[1], (TILES_X, half_axis), 1, second_limit + 1)
    flipped = jax.random.randint(keys[2], (TILES_X, half_axis), 0, 2) == 1
    lower = jnp.where(flipped, second, first)
    upper = jnp.where(flipped, first, second)
    chosen_row = jax.random.randint(keys[3], (), 0, TILES_X)
    chosen_pair = jax.random.randint(keys[4], (), 0, half_axis)
    grid_row = jnp.arange(TILES_X, dtype=jnp.int32)[:, None]
    grid_pair = jnp.arange(half_axis, dtype=jnp.int32)[None, :]
    chosen = (grid_row == chosen_row) & (grid_pair == chosen_pair)
    lower = jnp.where(chosen, CAP, lower)
    upper = jnp.where(chosen, 2 * BAL - CAP, upper)
    return jnp.concatenate([lower, upper], axis=1).astype(jnp.int32)


def block_scale(rng, shape, pieces, least, top_value):
    factor_of, own = 1.0, jax.random.fold_in(rng, 6)
    for position, shards_of in pieces:
        heights = jnp.exp(jax.random.uniform(jax.random.fold_in(own, position), (shards_of,), jnp.float32, least / len(pieces), top_value / len(pieces)))
        factor_of = factor_of * jnp.repeat(heights, shape[position] // shards_of).reshape([-1 if axis == position else 1 for axis in range(len(shape))])
    return factor_of


def centred(stream_key, shape, scale, reach, cuts=(), kind=jnp.bfloat16):
    drawn = scale * jax.random.normal(stream_key, shape, jnp.float32)
    if cuts:
        drawn = drawn * block_scale(stream_key, shape, cuts, -0.22, 0.18)
    return jnp.clip(drawn, -reach, reach).astype(kind)


def setup_inputs(seed: int = 0) -> dict:
    key_of = jax.random.split(jax.random.key(seed), 6)
    return {
        "object_field": centred(key_of[0], (2, OX, OY), 1.0, 6.0, ((1, 4), (2, 4)), jnp.float32),
        "probe": centred(key_of[1], (2, MODES, PS, PS), 0.5, 3.0, ((1, 2),), jnp.float32),
        "offsets": draw_offsets(jax.random.fold_in(key_of[5], 71), 0),
        "counts": draw_counts(jax.random.fold_in(key_of[5], 71), 0),
        "amplitude": jnp.clip(0.5 + 2.5 * jax.random.uniform(key_of[4], (TILES_X, TILES_Y, CAP, PS, PS), jnp.float32) ** block_scale(key_of[4], (TILES_X, TILES_Y, CAP, PS, PS), ((0, 4), (1, 4)), -0.2, 0.2), 0.5, 3.0),
    }


def reference(object_field, probe, offsets, counts, amplitude):
    modes_c = probe[0] + 1j * probe[1]
    tile_total = TILES_X * TILES_Y
    corner_all = offsets.reshape(tile_total, CAP, 2)
    count_all = counts.reshape(tile_total)
    measured_all = amplitude.reshape(tile_total, CAP, PS, PS)
    tile_ids = jnp.arange(tile_total, dtype=jnp.int32)
    zero_index = jnp.zeros((), jnp.int32)

    def tile_step(carry, inputs):
        grad_field, grad_probe = carry
        tile_id, corners, live_count, measured = inputs
        row_start = (tile_id // TILES_Y * TR + corners[:, 0]).astype(jnp.int32)
        col_start = (tile_id % TILES_Y * TC + corners[:, 1]).astype(jnp.int32)

        def take_one(row_first, col_first):
            return lax.dynamic_slice(object_field, (zero_index, row_first, col_first), (2, PS, PS))
        patches = jax.vmap(take_one)(row_start, col_start)
        patch_c = patches[:, 0] + 1j * patches[:, 1]
        exit_wave = modes_c[None] * patch_c[:, None]
        far = jnp.fft.fft2(exit_wave, norm='ortho')
        power = lax.optimization_barrier(jnp.sum(far.real * far.real + far.imag * far.imag, axis=1))
        live = (jnp.arange(CAP, dtype=jnp.int32) < live_count).astype(object_field.dtype)
        factor = live[:, None, None] * (1.0 - measured / jnp.sqrt(jnp.maximum(power, 0.25)))
        back = jnp.fft.ifft2(far * factor[:, None], norm='ortho')
        grad_probe = grad_probe + lax.optimization_barrier(jnp.sum(jnp.conj(patch_c)[:, None] * back, axis=0))
        patch_grad = lax.optimization_barrier(jnp.sum(jnp.conj(modes_c)[None] * back, axis=1))
        grad_parts = jnp.stack([patch_grad.real, patch_grad.imag], axis=1)

        def add_one(index_slot, accum):
            start = (zero_index, row_start[index_slot], col_start[index_slot])
            current = lax.dynamic_slice(accum, start, (2, PS, PS))
            return lax.dynamic_update_slice(accum, current + grad_parts[index_slot], start)
        grad_field = lax.fori_loop(0, CAP, add_one, grad_field)
        return ((grad_field, grad_probe), None)
    start_carry = (jnp.zeros_like(object_field), jnp.zeros(modes_c.shape, modes_c.dtype))
    final_carry, unused = lax.scan(tile_step, start_carry, (tile_ids, corner_all, count_all, measured_all))
    grad_field, grad_probe = final_carry
    return (grad_field, jnp.stack([grad_probe.real, grad_probe.imag]))
```

```python
import functools

import jax
import jax.numpy as jnp
import ml_dtypes
import numpy as np
from jax import lax
from jax.experimental import pallas as pl
from jax.experimental.pallas import tpu as pltpu
from jax.sharding import PartitionSpec as P

F32 = jnp.float32
BF16 = jnp.bfloat16
MESH = pl.DeviceIdType.MESH
VM = pl.BlockSpec(memory_space=pltpu.VMEM)
ANY = pl.BlockSpec(memory_space=pl.ANY)


def tables(side):
    half = side // 2
    line = np.arange(half)
    found = []
    for odd in (0, 1):
        product = (2 * line[:, None] + odd) * line[None, :] % side
        value = np.exp(-2j * np.pi * product / side) / np.sqrt(side)
        block = np.block([[value.real, -value.imag], [value.imag, value.real]])
        found.append(block)

    def parts(block):
        high = block.astype(np.float32).astype(ml_dtypes.bfloat16)
        low = (block - high.astype(np.float64)).astype(np.float32).astype(ml_dtypes.bfloat16)
        return high, high, low

    tall = [np.concatenate(parts(b), 0) for b in (found[0].T, found[1].T, found[0], found[1])]
    wide = [np.concatenate(parts(b), 1) for b in (found[0], found[1], found[0].T, found[1].T)]
    order = np.concatenate([np.arange(0, side, 2), np.arange(1, side, 2)])
    pick = np.zeros((side, side), np.float32)
    pick[order, np.arange(side)] = 1.0
    picks = np.stack([pick, pick.T]).astype(ml_dtypes.bfloat16)
    return np.stack(tall), np.stack(wide), picks


def split(x):
    high = x.astype(BF16)
    return high, (x - high.astype(F32)).astype(BF16)


def right_mul(x, table):
    high, low = split(x)
    return jnp.dot(jnp.concatenate([high, low, high], 1), table, preferred_element_type=F32)


def left_mul(table, x):
    high, low = split(x)
    return jnp.dot(table, jnp.concatenate([high, low, high], 0), preferred_element_type=F32)


def solve_kernel(off_ref, cnt_ref, core_ref, ext_ref, probe_ref, amp_ref, tall_ref, wide_ref, pick_ref,
                 grad_ref, pg_ref, far_e, far_o):
    step = pl.program_id(0)
    modes, side = probe_ref.shape[1], probe_ref.shape[2]
    half = side // 2
    slot = 2 * step + core_ref[0]

    @pl.when(step == 0)
    def _():
        grad_ref[...] = jnp.zeros_like(grad_ref)
        pg_ref[...] = jnp.zeros_like(pg_ref)

    @pl.when(slot < cnt_ref[0])
    def _():
        row = off_ref[slot, 0]
        col = off_ref[slot, 1]
        base = pl.multiple_of(col // 128 * 128, 128)
        shift = col - base
        width = side + 128
        top_row = pl.multiple_of(row // 8 * 8, 8)
        drop = row - top_row
        tall = side + 8
        window = (pl.ds(top_row, tall), pl.ds(base, width))

        def take(part):
            wide = ext_ref[(part, *window)]
            wide = pltpu.roll(wide, lax.rem(width - shift, width), 1)[:, :side]
            return pltpu.roll(wide, lax.rem(tall - drop, tall), 0)[:side]

        a_re, a_im = take(0), take(1)
        pow_e = pow_o = jnp.zeros((half, side), F32)
        for m in range(modes):
            p_re, p_im = probe_ref[0, m], probe_ref[1, m]
            e_re = p_re * a_re - p_im * a_im
            e_im = p_re * a_im + p_im * a_re
            x_e = jnp.concatenate([e_re[:, :half] + e_re[:, half:], e_im[:, :half] + e_im[:, half:]], 1)
            x_o = jnp.concatenate([e_re[:, :half] - e_re[:, half:], e_im[:, :half] - e_im[:, half:]], 1)
            z_e = right_mul(x_e, tall_ref[0])
            z_o = right_mul(x_o, tall_ref[1])
            z_re = jnp.concatenate([z_e[:, :half], z_o[:, :half]], 1)
            z_im = jnp.concatenate([z_e[:, half:], z_o[:, half:]], 1)
            y_e = jnp.concatenate([z_re[:half] + z_re[half:], z_im[:half] + z_im[half:]], 0)
            y_o = jnp.concatenate([z_re[:half] - z_re[half:], z_im[:half] - z_im[half:]], 0)
            f_e = left_mul(wide_ref[0], y_e)
            f_o = left_mul(wide_ref[1], y_o)
            far_e[m] = f_e
            far_o[m] = f_o
            pow_e = pow_e + (f_e[:half] * f_e[:half] + f_e[half:] * f_e[half:])
            pow_o = pow_o + (f_o[:half] * f_o[:half] + f_o[half:] * f_o[half:])
        measured = jnp.zeros((side, side), F32)
        for term in split(amp_ref[0]):
            moved = jnp.dot(term, pick_ref[0], preferred_element_type=F32).astype(BF16)
            measured = measured + jnp.dot(pick_ref[1], moved, preferred_element_type=F32)
        fac_e = 1.0 - measured[:half] * lax.rsqrt(jnp.maximum(pow_e, 0.25))
        fac_o = 1.0 - measured[half:] * lax.rsqrt(jnp.maximum(pow_o, 0.25))
        fac_e = jnp.concatenate([fac_e, fac_e], 0)
        fac_o = jnp.concatenate([fac_o, fac_o], 0)
        g_re = g_im = jnp.zeros((side, side), F32)
        for m in range(modes):
            q_e = left_mul(wide_ref[2], far_e[m] * fac_e)
            q_o = left_mul(wide_ref[3], far_o[m] * fac_o)
            top, low = q_e + q_o, q_e - q_o
            w_re = jnp.concatenate([top[:half], low[:half]], 0)
            w_im = jnp.concatenate([top[half:], low[half:]], 0)
            s_e = right_mul(jnp.concatenate([w_re[:, :half], w_im[:, :half]], 1), tall_ref[2])
            s_o = right_mul(jnp.concatenate([w_re[:, half:], w_im[:, half:]], 1), tall_ref[3])
            first, second = s_e + s_o, s_e - s_o
            b_re = jnp.concatenate([first[:, :half], second[:, :half]], 1)
            b_im = jnp.concatenate([first[:, half:], second[:, half:]], 1)
            pg_ref[0, m] += a_re * b_re + a_im * b_im
            pg_ref[1, m] += a_re * b_im - a_im * b_re
            p_re, p_im = probe_ref[0, m], probe_ref[1, m]
            g_re = g_re + (p_re * b_re + p_im * b_im)
            g_im = g_im + (p_re * b_im - p_im * b_re)
        for part, value in ((0, g_re), (1, g_im)):
            long = pltpu.roll(jnp.concatenate([value, jnp.zeros((8, side), F32)], 0), drop, 0)
            wide = jnp.concatenate([long, jnp.zeros((tall, 128), F32)], 1)
            grad_ref[(part, *window)] += pltpu.roll(wide, shift, 1)


def remote(src, dst, send, recv, where):
    return pltpu.make_async_remote_copy(src_ref=src, dst_ref=dst, send_sem=send, recv_sem=recv,
                                        device_id=where, device_id_type=MESH)


def greet(barrier, where):
    pl.semaphore_signal(barrier, inc=1, device_id=where, device_id_type=MESH)


def halo_kernel(nx, ny, obj, probe, ext, full, send, recv, own):
    u, v, m = lax.axis_index("gx"), lax.axis_index("gy"), lax.axis_index("ma")
    side = probe.shape[2]
    rows, cols = obj.shape[1], obj.shape[2]
    pm = probe.shape[1]
    other = (u, v, 1 - m)
    keep = [
        pltpu.make_async_copy(obj, ext.at[:, :rows, :cols], own.at[0]),
        pltpu.make_async_copy(probe, full.at[:, pl.ds(m * pm, pm)], own.at[1]),
    ]
    for c in keep:
        c.start()
    links = [
        (v > 0, v < ny - 1, (u, v - 1, m), (u, v + 1, m)),
        (u > 0, u < nx - 1, (u - 1, v, m), (u + 1, v, m)),
        ((u > 0) & (v > 0), (u < nx - 1) & (v < ny - 1), (u - 1, v - 1, m), (u + 1, v + 1, m)),
    ]
    barrier = pltpu.get_barrier_semaphore()
    greet(barrier, other)
    for goes, comes, target, source in links:
        @pl.when(goes)
        def _():
            greet(barrier, target)

        @pl.when(comes)
        def _():
            greet(barrier, source)
    count = lambda flag: jnp.where(flag, 1, 0)
    pl.semaphore_wait(barrier, 1 + sum(count(goes) + count(comes) for goes, comes, _, _ in links))

    def piece(ref, r0, rn, c0, cn):
        return ref.at[m, r0:r0 + rn, c0:c0 + cn]

    h = rows // 2
    pieces = [
        (0, (0, h, 0, side), (0, h, cols, side)),
        (1, (0, side, 0, cols), (rows, side, 0, cols)),
        (0, (h, h, 0, side), (h, h, cols, side)),
        (2, (0, side, 0, side), (rows, side, cols, side)),
    ]
    outs = []
    for n, (link, src, dst) in enumerate(pieces):
        goes, comes, target, source = links[link]
        c = remote(piece(obj, *src), piece(ext, *dst), send.at[n], recv.at[n], target)
        outs.append(c)

        @pl.when(goes)
        def _(c=c):
            c.start()
    mine = pl.ds(m * pm, pm)
    pc = remote(probe, full.at[:, mine], send.at[8], recv.at[8], other)
    pc.start()
    fwds = []
    for n, (link, src, dst) in enumerate(pieces):
        goes, comes, target, source = links[link]
        f = remote(piece(ext, *dst), piece(ext, *dst), send.at[4 + n], recv.at[4 + n], other)
        fwds.append(f)

        @pl.when(comes)
        def _(c=outs[n], f=f):
            c.wait_recv()
            f.start()
    for n, (link, src, dst) in enumerate(pieces):
        goes, comes, target, source = links[link]

        @pl.when(goes)
        def _(c=outs[n]):
            c.wait_send()

        @pl.when(comes)
        def _(f=fwds[n]):
            f.wait()
    pc.wait()
    for c in keep:
        c.wait()


def reduce_kernel(nx, ny, grad, pg, out, pout, rt_r, rt_l, rl, rp, low, edge, r_r, r_b, r_d,
                  acc, rx, px, ry, py, send, recv):
    u, v, m = lax.axis_index("gx"), lax.axis_index("gy"), lax.axis_index("ma")
    side = pg.shape[2]
    rows, cols = out.shape[1], out.shape[2]
    total = rows * 2
    pm = pg.shape[1] // 2
    o = 1 - m
    other = (u, v, o)
    last_x, last_y = nx - 1, ny - 1
    barrier = pltpu.get_barrier_semaphore()
    greet(barrier, other)
    for d in range(1, nx):
        greet(barrier, (lax.rem(u + d, nx), v, m))
        greet(barrier, (lax.rem(u + d, nx), v, o))
    for d in range(1, ny):
        greet(barrier, (u, lax.rem(v + d, ny), m))
    peers = 2 * nx + ny - 2
    corners = [((u < last_x) & (v < last_y), (u + 1, v + 1)), ((u > 0) & (v > 0), (u - 1, v - 1))]
    for there, (a, b) in corners:
        peers = peers + jnp.where(there, 2, 0)

        @pl.when(there)
        def _(a=a, b=b):
            greet(barrier, (a, b, 0))
            greet(barrier, (a, b, 1))
    pl.semaphore_wait(barrier, peers)

    theirs = pl.ds(pl.multiple_of(o * rows, 8), rows)
    mine = pl.ds(pl.multiple_of(m * rows, 8), rows)
    swaps = [
        remote(pg.at[:, pl.ds(o * pm, pm)], rp, send.at[0], recv.at[0], other),
        remote(grad.at[o, total:total + side, :], rl, send.at[1], recv.at[1], other),
        remote(grad.at[:, theirs, cols:cols + side], rt_r, send.at[2], recv.at[2], other),
        remote(grad.at[:, theirs, 0:cols], rt_l, send.at[3], recv.at[3], other),
    ]
    for c in swaps:
        c.start()
    swaps[0].wait_recv()
    for a in range(2):
        for b in range(pm):
            at = (a * pm + b) * side
            acc[at:at + side, :] = pg[a, m * pm + b] + rp[a, b]
    big = acc.shape[0] // nx
    small = big // ny
    gx_rs = []
    for d in range(1, nx):
        to = lax.rem(u + d, nx)
        c = remote(acc.at[pl.ds(pl.multiple_of(to * big, 8), big)], rx.at[d - 1], send.at[7 + d], recv.at[7 + d],
                   (to, v, m))
        c.start()
        gx_rs.append(c)
    swaps[1].wait_recv()
    low[...] = grad[m, total:total + side, :] + rl[...]
    c_b = remote(low.at[:, 0:cols], r_b.at[m], send.at[4], recv.at[4 + m], (u + 1, v, 0))
    c_d = remote(low.at[:, cols:cols + side], r_d.at[m], send.at[5], recv.at[6 + m], (u + 1, v + 1, 0))
    c_r = remote(edge, r_r, send.at[6], recv.at[3 + 5 + 2 * nx], (u, v + 1, m))

    @pl.when(u < last_x)
    def _():
        c_b.start()

    @pl.when((u < last_x) & (v < last_y))
    def _():
        c_d.start()
    swaps[2].wait_recv()
    edge[...] = grad[:, mine, cols:cols + side] + rt_r[...]

    @pl.when(v < last_y)
    def _():
        c_r.start()
    for c in gx_rs:
        c.wait_recv()
    px[...] = acc[pl.ds(pl.multiple_of(u * big, 8), big), :]
    for d in range(1, nx):
        px[...] += rx[d - 1]
    base = 9 + 2 * nx
    gy_rs = []
    for d in range(1, ny):
        to = lax.rem(v + d, ny)
        c = remote(px.at[pl.ds(pl.multiple_of(to * small, 8), small)], ry.at[d - 1], send.at[base + d],
                   recv.at[base + d], (u, to, m))
        c.start()
        gy_rs.append(c)
    swaps[3].wait_recv()
    out[...] = grad[:, mine, 0:cols] + rt_l[...]
    for c in gy_rs:
        c.wait_recv()
    here = pl.ds(pl.multiple_of(u * big + v * small, 8), small)
    part = px[pl.ds(pl.multiple_of(v * small, 8), small), :]
    for d in range(1, ny):
        part = part + ry[d - 1]
    py[...] = part
    pout[here, :] = part
    base = base + ny
    gy_ag = []
    for d in range(1, ny):
        to = lax.rem(v + d, ny)
        c = remote(py, pout.at[here], send.at[base + d], recv.at[base + d], (u, to, m))
        c.start()
        gy_ag.append(c)
    for c in gy_ag:
        c.wait_recv()
    band = pl.ds(pl.multiple_of(u * big, 8), big)
    gx_ag = []
    for d in range(1, nx):
        to = lax.rem(u + d, nx)
        c = remote(pout.at[band], pout.at[band], send.at[7 + nx + d], recv.at[7 + nx + d], (to, v, m))
        c.start()
        gx_ag.append(c)

    @pl.when(v > 0)
    def _():
        c_r.wait_recv()
        out[:, :, 0:side] += r_r[...]

    @pl.when((u > 0) & (m == 0))
    def _():
        for k in range(2):
            remote(low.at[:, 0:cols], r_b.at[k], send.at[4], recv.at[4 + k], other).wait_recv()
        out[:, 0:side, :] += r_b[...]

    @pl.when((u > 0) & (v > 0) & (m == 0))
    def _():
        for k in range(2):
            remote(low.at[:, cols:cols + side], r_d.at[k], send.at[5], recv.at[6 + k], other).wait_recv()
        out[:, 0:side, 0:side] += r_d[...]
    for c in gx_ag:
        c.wait_recv()
    for c in swaps + gx_rs + gy_rs + gy_ag + gx_ag:
        c.wait_send()

    @pl.when(u < last_x)
    def _():
        c_b.wait_send()

    @pl.when((u < last_x) & (v < last_y))
    def _():
        c_d.wait_send()

    @pl.when(v < last_y)
    def _():
        c_r.wait_send()


def local(nx, ny, object_field, probe, offsets, counts, amplitude):
    side = probe.shape[2]
    own_modes = probe.shape[1]
    modes = own_modes * 2
    rows, cols = object_field.shape[1:]
    cap = offsets.shape[2]
    dma = pltpu.SemaphoreType.DMA
    ext, full = pl.pallas_call(
        functools.partial(halo_kernel, nx, ny),
        name="halo",
        out_shape=(jax.ShapeDtypeStruct((2, rows + side, cols + side), F32),
                   jax.ShapeDtypeStruct((2, modes, side, side), F32)),
        in_specs=[ANY, ANY],
        out_specs=(ANY, ANY),
        scratch_shapes=[dma((9,)), dma((9,)), dma((2,))],
        compiler_params=pltpu.CompilerParams(collective_id=0, has_side_effects=True),
    )(object_field, probe)
    tall, wide, picks = tables(side)
    core = lax.axis_index("ma").astype(jnp.int32).reshape(1)
    whole = lambda shape: pl.BlockSpec(shape, lambda i, *_: (0,) * len(shape), pipeline_mode=pl.Buffered(1))
    grad, pg = pl.pallas_call(
        solve_kernel,
        name="solve",
        out_shape=(jax.ShapeDtypeStruct(ext.shape, F32), jax.ShapeDtypeStruct(full.shape, F32)),
        grid_spec=pltpu.PrefetchScalarGridSpec(
            num_scalar_prefetch=3,
            grid=(cap // 2,),
            in_specs=[
                whole(ext.shape), whole(full.shape),
                pl.BlockSpec((1, side, side), lambda i, off, cnt, core: (2 * i + core[0], 0, 0)),
                whole(tall.shape), whole(wide.shape), whole(picks.shape),
            ],
            out_specs=(whole(ext.shape), whole(full.shape)),
            scratch_shapes=[pltpu.VMEM((modes, side, side), F32), pltpu.VMEM((modes, side, side), F32)],
        ),
        compiler_params=pltpu.CompilerParams(vmem_limit_bytes=48 << 20),
    )(offsets[0, 0], counts[0], core, ext, full, amplitude[0, 0],
      jnp.asarray(tall), jnp.asarray(wide), jnp.asarray(picks))
    half = rows // 2
    flat = 2 * own_modes * side
    big = flat // nx
    nsem = 9 + 2 * nx + 2 * ny + 2
    object_grad, probe_grad = pl.pallas_call(
        functools.partial(reduce_kernel, nx, ny),
        name="reduce",
        out_shape=(jax.ShapeDtypeStruct((2, half, cols), F32), jax.ShapeDtypeStruct((flat, side), F32)),
        in_specs=[VM, VM],
        out_specs=(VM, VM),
        scratch_shapes=[
            pltpu.VMEM((2, half, side), F32), pltpu.VMEM((2, half, cols), F32),
            pltpu.VMEM((side, cols + side), F32), pltpu.VMEM((2, own_modes, side, side), F32),
            pltpu.VMEM((side, cols + side), F32), pltpu.VMEM((2, half, side), F32),
            pltpu.VMEM((2, half, side), F32), pltpu.VMEM((2, side, cols), F32), pltpu.VMEM((2, side, side), F32),
            pltpu.VMEM((flat, side), F32), pltpu.VMEM((nx - 1, big, side), F32), pltpu.VMEM((big, side), F32),
            pltpu.VMEM((ny - 1, big // ny, side), F32), pltpu.VMEM((big // ny, side), F32),
            dma((nsem,)), dma((nsem,)),
        ],
        compiler_params=pltpu.CompilerParams(collective_id=1, has_side_effects=True, vmem_limit_bytes=48 << 20),
    )(grad, pg)
    return object_grad, probe_grad.reshape(2, own_modes, side, side)


def solution(mesh):
    return jax.shard_map(
        functools.partial(local, mesh.shape["gx"], mesh.shape["gy"]),
        mesh=mesh,
        in_specs=(
            P(None, "gx", "gy"),
            P(None, "ma", None, None),
            P("gx", "gy", None, None),
            P("gx", "gy"),
            P("gx", "gy", None, None, None),
        ),
        out_specs=(P(None, ("gx", "ma"), "gy"), P(None, "ma", None, None)),
        check_vma=False,
    )
```

```python
import functools

import jax
import jax.numpy as jnp
import ml_dtypes
import numpy as np
from jax import lax
from jax.experimental import pallas as pl
from jax.experimental.pallas import tpu as pltpu
from jax.sharding import PartitionSpec as P

F32 = jnp.float32
BF16 = jnp.bfloat16
MESH = pl.DeviceIdType.MESH
VM = pl.BlockSpec(memory_space=pltpu.VMEM)


def tables(side):
    half = side // 2
    line = np.arange(half)
    found = []
    for odd in (0, 1):
        product = (2 * line[:, None] + odd) * line[None, :] % side
        value = np.exp(-2j * np.pi * product / side) / np.sqrt(side)
        block = np.block([[value.real, -value.imag], [value.imag, value.real]])
        found.append(block)

    def parts(block):
        high = block.astype(np.float32).astype(ml_dtypes.bfloat16)
        low = (block - high.astype(np.float64)).astype(np.float32).astype(ml_dtypes.bfloat16)
        return high, high, low

    tall = [np.concatenate(parts(b), 0) for b in (found[0].T, found[1].T, found[0], found[1])]
    wide = [np.concatenate(parts(b), 1) for b in (found[0], found[1], found[0].T, found[1].T)]
    order = np.concatenate([np.arange(0, side, 2), np.arange(1, side, 2)])
    pick = np.zeros((side, side), np.float32)
    pick[order, np.arange(side)] = 1.0
    picks = np.stack([pick, pick.T]).astype(ml_dtypes.bfloat16)
    return np.stack(tall), np.stack(wide), picks


def split(x):
    high = x.astype(BF16)
    return high, (x - high.astype(F32)).astype(BF16)


def right_mul(x, table):
    high, low = split(x)
    return jnp.dot(jnp.concatenate([high, low, high], 1), table, preferred_element_type=F32)


def left_mul(table, x):
    high, low = split(x)
    return jnp.dot(table, jnp.concatenate([high, low, high], 0), preferred_element_type=F32)


def solve_kernel(off_ref, cnt_ref, core_ref, ext_ref, probe_ref, amp_ref, tall_ref, wide_ref, pick_ref,
                 grad_ref, pg_ref, far_e, far_o):
    step = pl.program_id(0)
    modes, side = probe_ref.shape[1], probe_ref.shape[2]
    half = side // 2
    slot = 2 * step + core_ref[0]

    @pl.when(step == 0)
    def _():
        grad_ref[...] = jnp.zeros_like(grad_ref)
        pg_ref[...] = jnp.zeros_like(pg_ref)

    @pl.when(slot < cnt_ref[0])
    def _():
        row = off_ref[slot, 0]
        col = off_ref[slot, 1]
        base = pl.multiple_of(col // 128 * 128, 128)
        shift = col - base
        width = side + 128
        top_row = pl.multiple_of(row // 8 * 8, 8)
        drop = row - top_row
        tall = side + 8
        window = (pl.ds(top_row, tall), pl.ds(base, width))

        def take(part):
            wide = ext_ref[(part, *window)]
            wide = pltpu.roll(wide, lax.rem(width - shift, width), 1)[:, :side]
            return pltpu.roll(wide, lax.rem(tall - drop, tall), 0)[:side]

        a_re, a_im = take(0), take(1)
        pow_e = pow_o = jnp.zeros((half, side), F32)
        for m in range(modes):
            p_re, p_im = probe_ref[0, m], probe_ref[1, m]
            e_re = p_re * a_re - p_im * a_im
            e_im = p_re * a_im + p_im * a_re
            x_e = jnp.concatenate([e_re[:, :half] + e_re[:, half:], e_im[:, :half] + e_im[:, half:]], 1)
            x_o = jnp.concatenate([e_re[:, :half] - e_re[:, half:], e_im[:, :half] - e_im[:, half:]], 1)
            z_e = right_mul(x_e, tall_ref[0])
            z_o = right_mul(x_o, tall_ref[1])
            z_re = jnp.concatenate([z_e[:, :half], z_o[:, :half]], 1)
            z_im = jnp.concatenate([z_e[:, half:], z_o[:, half:]], 1)
            y_e = jnp.concatenate([z_re[:half] + z_re[half:], z_im[:half] + z_im[half:]], 0)
            y_o = jnp.concatenate([z_re[:half] - z_re[half:], z_im[:half] - z_im[half:]], 0)
            f_e = left_mul(wide_ref[0], y_e)
            f_o = left_mul(wide_ref[1], y_o)
            far_e[m] = f_e
            far_o[m] = f_o
            pow_e = pow_e + (f_e[:half] * f_e[:half] + f_e[half:] * f_e[half:])
            pow_o = pow_o + (f_o[:half] * f_o[:half] + f_o[half:] * f_o[half:])
        measured = jnp.zeros((side, side), F32)
        for term in split(amp_ref[0]):
            moved = jnp.dot(term, pick_ref[0], preferred_element_type=F32).astype(BF16)
            measured = measured + jnp.dot(pick_ref[1], moved, preferred_element_type=F32)
        fac_e = 1.0 - measured[:half] * lax.rsqrt(jnp.maximum(pow_e, 0.25))
        fac_o = 1.0 - measured[half:] * lax.rsqrt(jnp.maximum(pow_o, 0.25))
        fac_e = jnp.concatenate([fac_e, fac_e], 0)
        fac_o = jnp.concatenate([fac_o, fac_o], 0)
        g_re = g_im = jnp.zeros((side, side), F32)
        for m in range(modes):
            q_e = left_mul(wide_ref[2], far_e[m] * fac_e)
            q_o = left_mul(wide_ref[3], far_o[m] * fac_o)
            top, low = q_e + q_o, q_e - q_o
            w_re = jnp.concatenate([top[:half], low[:half]], 0)
            w_im = jnp.concatenate([top[half:], low[half:]], 0)
            s_e = right_mul(jnp.concatenate([w_re[:, :half], w_im[:, :half]], 1), tall_ref[2])
            s_o = right_mul(jnp.concatenate([w_re[:, half:], w_im[:, half:]], 1), tall_ref[3])
            first, second = s_e + s_o, s_e - s_o
            b_re = jnp.concatenate([first[:, :half], second[:, :half]], 1)
            b_im = jnp.concatenate([first[:, half:], second[:, half:]], 1)
            pg_ref[0, m] += a_re * b_re + a_im * b_im
            pg_ref[1, m] += a_re * b_im - a_im * b_re
            p_re, p_im = probe_ref[0, m], probe_ref[1, m]
            g_re = g_re + (p_re * b_re + p_im * b_im)
            g_im = g_im + (p_re * b_im - p_im * b_re)
        for part, value in ((0, g_re), (1, g_im)):
            long = pltpu.roll(jnp.concatenate([value, jnp.zeros((8, side), F32)], 0), drop, 0)
            wide = jnp.concatenate([long, jnp.zeros((tall, 128), F32)], 1)
            grad_ref[(part, *window)] += pltpu.roll(wide, shift, 1)


def remote(src, dst, send, recv, where):
    return pltpu.make_async_remote_copy(src_ref=src, dst_ref=dst, send_sem=send, recv_sem=recv,
                                        device_id=where, device_id_type=MESH)


def greet(barrier, where):
    pl.semaphore_signal(barrier, inc=1, device_id=where, device_id_type=MESH)


def halo_kernel(nx, ny, obj, probe, ext, full, send, recv):
    u, v, m = lax.axis_index("gx"), lax.axis_index("gy"), lax.axis_index("ma")
    side = probe.shape[2]
    rows, cols = obj.shape[1], obj.shape[2]
    pm = probe.shape[1]
    other = (u, v, 1 - m)
    right, below = v < ny - 1, u < nx - 1
    left_dev, right_dev = (u, v - 1, m), (u, v + 1, m)
    up_dev, down_dev = (u - 1, v, m), (u + 1, v, m)
    barrier = pltpu.get_barrier_semaphore()
    greet(barrier, other)
    peers = 1
    for there, where in ((v > 0, left_dev), (right, right_dev), (u > 0, up_dev), (below, down_dev)):
        peers = peers + jnp.where(there, 1, 0)

        @pl.when(there)
        def _(where=where):
            greet(barrier, where)
    pl.semaphore_wait(barrier, peers)

    def piece(ref, r0, rn, c0, cn):
        return ref.at[m, r0:r0 + rn, c0:c0 + cn]

    h = rows - side
    first, rest = (0, side, cols, side), (side, h, cols, side)
    under, corner = (rows, side, 0, cols), (rows, side, cols, side)
    hops = [
        (piece(obj, 0, side, 0, side), first, v > 0, right, left_dev),
        (piece(obj, 0, side, 0, cols), under, u > 0, below, up_dev),
        (piece(obj, side, h, 0, side), rest, v > 0, right, left_dev),
        (piece(ext, *first), corner, (u > 0) & right, below & right, up_dev),
    ]
    outs, fwds = [], []
    for n, (src, place, goes, comes, target) in enumerate(hops):
        outs.append(remote(src, piece(ext, *place), send.at[n], recv.at[n], target))
        fwds.append(remote(piece(ext, *place), piece(ext, *place), send.at[4 + n], recv.at[4 + n], other))
    for n in range(3):
        @pl.when(hops[n][2])
        def _(n=n):
            outs[n].start()
    mine = pl.ds(m * pm, pm)
    pc = remote(probe, full.at[:, mine], send.at[8], recv.at[8], other)
    pc.start()
    ext[:, 0:rows, 0:cols] = obj[...]
    full[:, mine] = probe[...]
    for n, (src, place, goes, comes, target) in enumerate(hops):
        @pl.when(comes)
        def _(n=n):
            outs[n].wait_recv()
            if n == 0:
                @pl.when(u > 0)
                def _():
                    outs[3].start()
            fwds[n].start()
    for n, (src, place, goes, comes, target) in enumerate(hops):
        @pl.when(goes)
        def _(n=n):
            outs[n].wait_send()

        @pl.when(comes)
        def _(n=n):
            fwds[n].wait()
    pc.wait()


def reduce_kernel(nx, ny, grad, pg, out, pout, rt_r, rt_l, rl, rp, low, edge, r_r, r_b, r_d,
                  acc, rx, px, ry, py, send, recv):
    u, v, m = lax.axis_index("gx"), lax.axis_index("gy"), lax.axis_index("ma")
    side = pg.shape[2]
    rows, cols = out.shape[1], out.shape[2]
    total = rows * 2
    pm = pg.shape[1] // 2
    o = 1 - m
    other = (u, v, o)
    last_x, last_y = nx - 1, ny - 1
    barrier = pltpu.get_barrier_semaphore()
    greet(barrier, other)
    for d in range(1, nx):
        greet(barrier, (lax.rem(u + d, nx), v, m))
        greet(barrier, (lax.rem(u + d, nx), v, o))
    for d in range(1, ny):
        greet(barrier, (u, lax.rem(v + d, ny), m))
    peers = 2 * nx + ny - 2
    pl.semaphore_wait(barrier, peers)

    theirs = pl.ds(pl.multiple_of(o * rows, 8), rows)
    mine = pl.ds(pl.multiple_of(m * rows, 8), rows)
    swaps = [
        remote(pg.at[:, pl.ds(o * pm, pm)], rp, send.at[0], recv.at[0], other),
        remote(grad.at[o, total:total + side, :], rl, send.at[1], recv.at[1], other),
        remote(grad.at[:, theirs, cols:cols + side], rt_r, send.at[2], recv.at[2], other),
        remote(grad.at[:, theirs, 0:cols], rt_l, send.at[3], recv.at[3], other),
    ]
    for c in swaps:
        c.start()
    swaps[0].wait_recv()
    for a in range(2):
        for b in range(pm):
            at = (a * pm + b) * side
            acc[at:at + side, :] = pg[a, m * pm + b] + rp[a, b]
    big = acc.shape[0] // nx
    small = big // ny
    gx_rs = []
    for d in range(1, nx):
        to = lax.rem(u + d, nx)
        c = remote(acc.at[pl.ds(pl.multiple_of(to * big, 8), big)], rx.at[d - 1], send.at[7 + d], recv.at[7 + d],
                   (to, v, m))
        c.start()
        gx_rs.append(c)
    swaps[1].wait_recv()
    low[...] = grad[m, total:total + side, :] + rl[...]
    c_b = remote(low, r_b.at[m], send.at[4], recv.at[4 + m], (u + 1, v, 0))
    c_d = remote(r_b.at[:, :, cols:cols + side], r_d, send.at[5], recv.at[6], (u, v + 1, 0))
    c_r = remote(edge, r_r, send.at[6], recv.at[3 + 5 + 2 * nx], (u, v + 1, m))
    swaps[2].wait_recv()
    edge[...] = grad[:, mine, cols:cols + side] + rt_r[...]

    @pl.when(v < last_y)
    def _():
        c_r.start()
    for c in gx_rs:
        c.wait_recv()

    @pl.when(u < last_x)
    def _():
        c_b.start()
    px[...] = acc[pl.ds(pl.multiple_of(u * big, 8), big), :]
    for d in range(1, nx):
        px[...] += rx[d - 1]
    base = 9 + 2 * nx
    gy_rs = []
    for d in range(1, ny):
        to = lax.rem(v + d, ny)
        c = remote(px.at[pl.ds(pl.multiple_of(to * small, 8), small)], ry.at[d - 1], send.at[base + d],
                   recv.at[base + d], (u, to, m))
        c.start()
        gy_rs.append(c)
    swaps[3].wait_recv()
    out[...] = grad[:, mine, 0:cols] + rt_l[...]
    for c in gy_rs:
        c.wait_recv()
    here = pl.ds(pl.multiple_of(u * big + v * small, 8), small)
    part = px[pl.ds(pl.multiple_of(v * small, 8), small), :]
    for d in range(1, ny):
        part = part + ry[d - 1]
    py[...] = part
    pout[here, :] = part
    base = base + ny
    gy_ag = []
    for d in range(1, ny):
        to = lax.rem(v + d, ny)
        c = remote(py, pout.at[here], send.at[base + d], recv.at[base + d], (u, to, m))
        c.start()
        gy_ag.append(c)
    for c in gy_ag:
        c.wait_recv()
    band = pl.ds(pl.multiple_of(u * big, 8), big)
    gx_ag = []
    for d in range(1, nx):
        to = lax.rem(u + d, nx)
        c = remote(pout.at[band], pout.at[band], send.at[7 + nx + d], recv.at[7 + nx + d], (to, v, m))
        c.start()
        gx_ag.append(c)

    @pl.when(v > 0)
    def _():
        c_r.wait_recv()
        out[:, :, 0:side] += r_r[...]

    @pl.when((u > 0) & (m == 0))
    def _():
        for k in range(2):
            remote(low, r_b.at[k], send.at[4], recv.at[4 + k], other).wait_recv()

        @pl.when(v < last_y)
        def _():
            c_d.start()
        out[:, 0:side, :] += r_b[:, :, 0:cols]

        @pl.when(v > 0)
        def _():
            c_d.wait_recv()
            out[:, 0:side, 0:side] += r_d[...]
    for c in gx_ag:
        c.wait_recv()
    for c in swaps + gx_rs + gy_rs + gy_ag + gx_ag:
        c.wait_send()

    @pl.when(u < last_x)
    def _():
        c_b.wait_send()

    @pl.when((u > 0) & (v < last_y) & (m == 0))
    def _():
        c_d.wait_send()

    @pl.when(v < last_y)
    def _():
        c_r.wait_send()


def local(nx, ny, object_field, probe, offsets, counts, amplitude):
    side = probe.shape[2]
    own_modes = probe.shape[1]
    modes = own_modes * 2
    rows, cols = object_field.shape[1:]
    cap = offsets.shape[2]
    dma = pltpu.SemaphoreType.DMA
    ext, full = pl.pallas_call(
        functools.partial(halo_kernel, nx, ny),
        name="halo",
        out_shape=(jax.ShapeDtypeStruct((2, rows + side, cols + side), F32),
                   jax.ShapeDtypeStruct((2, modes, side, side), F32)),
        in_specs=[VM, VM],
        out_specs=(VM, VM),
        scratch_shapes=[dma((9,)), dma((9,))],
        compiler_params=pltpu.CompilerParams(collective_id=0, has_side_effects=True, vmem_limit_bytes=48 << 20),
    )(object_field, probe)
    tall, wide, picks = tables(side)
    core = lax.axis_index("ma").astype(jnp.int32).reshape(1)
    whole = lambda shape: pl.BlockSpec(shape, lambda i, *_: (0,) * len(shape), pipeline_mode=pl.Buffered(1))
    grad, pg = pl.pallas_call(
        solve_kernel,
        name="solve",
        out_shape=(jax.ShapeDtypeStruct(ext.shape, F32), jax.ShapeDtypeStruct(full.shape, F32)),
        grid_spec=pltpu.PrefetchScalarGridSpec(
            num_scalar_prefetch=3,
            grid=(cap // 2,),
            in_specs=[
                whole(ext.shape), whole(full.shape),
                pl.BlockSpec((1, side, side), lambda i, off, cnt, core: (2 * i + core[0], 0, 0)),
                whole(tall.shape), whole(wide.shape), whole(picks.shape),
            ],
            out_specs=(whole(ext.shape), whole(full.shape)),
            scratch_shapes=[pltpu.VMEM((modes, side, side), F32), pltpu.VMEM((modes, side, side), F32)],
        ),
        compiler_params=pltpu.CompilerParams(vmem_limit_bytes=48 << 20),
    )(offsets[0, 0], counts[0], core, ext, full, amplitude[0, 0],
      jnp.asarray(tall), jnp.asarray(wide), jnp.asarray(picks))
    half = rows // 2
    flat = 2 * own_modes * side
    big = flat // nx
    nsem = 9 + 2 * nx + 2 * ny + 2
    object_grad, probe_grad = pl.pallas_call(
        functools.partial(reduce_kernel, nx, ny),
        name="reduce",
        out_shape=(jax.ShapeDtypeStruct((2, half, cols), F32), jax.ShapeDtypeStruct((flat, side), F32)),
        in_specs=[VM, VM],
        out_specs=(VM, VM),
        scratch_shapes=[
            pltpu.VMEM((2, half, side), F32), pltpu.VMEM((2, half, cols), F32),
            pltpu.VMEM((side, cols + side), F32), pltpu.VMEM((2, own_modes, side, side), F32),
            pltpu.VMEM((side, cols + side), F32), pltpu.VMEM((2, half, side), F32),
            pltpu.VMEM((2, half, side), F32), pltpu.VMEM((2, side, cols + side), F32), pltpu.VMEM((2, side, side), F32),
            pltpu.VMEM((flat, side), F32), pltpu.VMEM((nx - 1, big, side), F32), pltpu.VMEM((big, side), F32),
            pltpu.VMEM((ny - 1, big // ny, side), F32), pltpu.VMEM((big // ny, side), F32),
            dma((nsem,)), dma((nsem,)),
        ],
        compiler_params=pltpu.CompilerParams(collective_id=1, has_side_effects=True, vmem_limit_bytes=48 << 20),
    )(grad, pg)
    return object_grad, probe_grad.reshape(2, own_modes, side, side)


def solution(mesh):
    return jax.shard_map(
        functools.partial(local, mesh.shape["gx"], mesh.shape["gy"]),
        mesh=mesh,
        in_specs=(
            P(None, "gx", "gy"),
            P(None, "ma", None, None),
            P("gx", "gy", None, None),
            P("gx", "gy"),
            P("gx", "gy", None, None, None),
        ),
        out_specs=(P(None, ("gx", "ma"), "gy"), P(None, "ma", None, None)),
        check_vma=False,
    )
```

```python
import functools

import jax
import jax.numpy as jnp
import ml_dtypes
import numpy as np
from jax import lax
from jax.experimental import pallas as pl
from jax.experimental.pallas import tpu as pltpu
from jax.sharding import PartitionSpec as P

F32 = jnp.float32
BF16 = jnp.bfloat16
MESH = pl.DeviceIdType.MESH
SM = pl.BlockSpec(memory_space=pltpu.SMEM)
VM = pl.BlockSpec(memory_space=pltpu.VMEM)


def tables(side):
    half = side // 2
    line = np.arange(half)
    found = []
    for odd in (0, 1):
        product = (2 * line[:, None] + odd) * line[None, :] % side
        value = np.exp(-2j * np.pi * product / side) / np.sqrt(side)
        block = np.block([[value.real, -value.imag], [value.imag, value.real]])
        found.append(block)

    def parts(block):
        high = block.astype(np.float32).astype(ml_dtypes.bfloat16)
        low = (block - high.astype(np.float64)).astype(np.float32).astype(ml_dtypes.bfloat16)
        return high, high, low

    tall = [np.concatenate(parts(b), 0) for b in (found[0].T, found[1].T, found[0], found[1])]
    wide = [np.concatenate(parts(b), 1) for b in (found[0], found[1], found[0].T, found[1].T)]
    order = np.concatenate([np.arange(0, side, 2), np.arange(1, side, 2)])
    pick = np.zeros((side, side), np.float32)
    pick[order, np.arange(side)] = 1.0
    picks = np.stack([pick, pick.T]).astype(ml_dtypes.bfloat16)
    return np.stack(tall), np.stack(wide), picks


def split(x):
    high = x.astype(BF16)
    return high, (x - high.astype(F32)).astype(BF16)


def right_mul(x, table):
    high, low = split(x)
    return jnp.dot(jnp.concatenate([high, low, high], 1), table, preferred_element_type=F32)


def left_mul(table, x):
    high, low = split(x)
    return jnp.dot(table, jnp.concatenate([high, low, high], 0), preferred_element_type=F32)


def solve_kernel(off_ref, cnt_ref, core_ref, ext_ref, probe_ref, amp_ref, tall_ref, wide_ref, pick_ref,
                 grad_ref, pg_ref, far_e, far_o):
    modes, side = probe_ref.shape[1], probe_ref.shape[2]
    half = side // 2
    grad_ref[...] = jnp.zeros_like(grad_ref)
    pg_ref[...] = jnp.zeros_like(pg_ref)

    @pl.loop(0, (cnt_ref[0] + 1 - core_ref[0]) // 2)
    def _(step):
        slot = 2 * step + core_ref[0]
        row = off_ref[slot, 0]
        col = off_ref[slot, 1]
        base = pl.multiple_of(col // 128 * 128, 128)
        shift = col - base
        width = side + 128
        top_row = pl.multiple_of(row // 8 * 8, 8)
        drop = row - top_row
        tall = side + 8
        window = (pl.ds(top_row, tall), pl.ds(base, width))

        def take(part):
            wide = ext_ref[(part, *window)]
            wide = pltpu.roll(wide, lax.rem(width - shift, width), 1)[:, :side]
            return pltpu.roll(wide, lax.rem(tall - drop, tall), 0)[:side]

        a_re, a_im = take(0), take(1)
        pow_e = pow_o = jnp.zeros((half, side), F32)
        for m in range(modes):
            p_re, p_im = probe_ref[0, m], probe_ref[1, m]
            e_re = p_re * a_re - p_im * a_im
            e_im = p_re * a_im + p_im * a_re
            x_e = jnp.concatenate([e_re[:, :half] + e_re[:, half:], e_im[:, :half] + e_im[:, half:]], 1)
            x_o = jnp.concatenate([e_re[:, :half] - e_re[:, half:], e_im[:, :half] - e_im[:, half:]], 1)
            z_e = right_mul(x_e, tall_ref[0])
            z_o = right_mul(x_o, tall_ref[1])
            z_re = jnp.concatenate([z_e[:, :half], z_o[:, :half]], 1)
            z_im = jnp.concatenate([z_e[:, half:], z_o[:, half:]], 1)
            y_e = jnp.concatenate([z_re[:half] + z_re[half:], z_im[:half] + z_im[half:]], 0)
            y_o = jnp.concatenate([z_re[:half] - z_re[half:], z_im[:half] - z_im[half:]], 0)
            f_e = left_mul(wide_ref[0], y_e)
            f_o = left_mul(wide_ref[1], y_o)
            far_e[m] = f_e
            far_o[m] = f_o
            pow_e = pow_e + (f_e[:half] * f_e[:half] + f_e[half:] * f_e[half:])
            pow_o = pow_o + (f_o[:half] * f_o[:half] + f_o[half:] * f_o[half:])
        measured = jnp.zeros((side, side), F32)
        for term in split(amp_ref[slot]):
            moved = jnp.dot(term, pick_ref[0], preferred_element_type=F32).astype(BF16)
            measured = measured + jnp.dot(pick_ref[1], moved, preferred_element_type=F32)
        fac_e = 1.0 - measured[:half] * lax.rsqrt(jnp.maximum(pow_e, 0.25))
        fac_o = 1.0 - measured[half:] * lax.rsqrt(jnp.maximum(pow_o, 0.25))
        fac_e = jnp.concatenate([fac_e, fac_e], 0)
        fac_o = jnp.concatenate([fac_o, fac_o], 0)
        g_re = g_im = jnp.zeros((side, side), F32)
        for m in range(modes):
            q_e = left_mul(wide_ref[2], far_e[m] * fac_e)
            q_o = left_mul(wide_ref[3], far_o[m] * fac_o)
            top, low = q_e + q_o, q_e - q_o
            w_re = jnp.concatenate([top[:half], low[:half]], 0)
            w_im = jnp.concatenate([top[half:], low[half:]], 0)
            s_e = right_mul(jnp.concatenate([w_re[:, :half], w_im[:, :half]], 1), tall_ref[2])
            s_o = right_mul(jnp.concatenate([w_re[:, half:], w_im[:, half:]], 1), tall_ref[3])
            first, second = s_e + s_o, s_e - s_o
            b_re = jnp.concatenate([first[:, :half], second[:, :half]], 1)
            b_im = jnp.concatenate([first[:, half:], second[:, half:]], 1)
            pg_ref[0, m] += a_re * b_re + a_im * b_im
            pg_ref[1, m] += a_re * b_im - a_im * b_re
            p_re, p_im = probe_ref[0, m], probe_ref[1, m]
            g_re = g_re + (p_re * b_re + p_im * b_im)
            g_im = g_im + (p_re * b_im - p_im * b_re)
        for part, value in ((0, g_re), (1, g_im)):
            long = pltpu.roll(jnp.concatenate([value, jnp.zeros((8, side), F32)], 0), drop, 0)
            wide = jnp.concatenate([long, jnp.zeros((tall, 128), F32)], 1)
            grad_ref[(part, *window)] += pltpu.roll(wide, shift, 1)


def remote(src, dst, send, recv, where):
    return pltpu.make_async_remote_copy(src_ref=src, dst_ref=dst, send_sem=send, recv_sem=recv,
                                        device_id=where, device_id_type=MESH)


def greet(barrier, where):
    pl.semaphore_signal(barrier, inc=1, device_id=where, device_id_type=MESH)


def halo_kernel(nx, ny, obj, probe, ext, full, send, recv):
    u, v, m = lax.axis_index("gx"), lax.axis_index("gy"), lax.axis_index("ma")
    side = probe.shape[2]
    rows, cols = obj.shape[1], obj.shape[2]
    pm = probe.shape[1]
    other = (u, v, 1 - m)
    right, below = v < ny - 1, u < nx - 1
    left_dev, right_dev = (u, v - 1, m), (u, v + 1, m)
    up_dev, down_dev = (u - 1, v, m), (u + 1, v, m)
    barrier = pltpu.get_barrier_semaphore()
    greet(barrier, other)
    peers = 1
    for there, where in ((v > 0, left_dev), (right, right_dev), (u > 0, up_dev), (below, down_dev)):
        peers = peers + jnp.where(there, 1, 0)

        @pl.when(there)
        def _(where=where):
            greet(barrier, where)
    pl.semaphore_wait(barrier, peers)

    def piece(ref, r0, rn, c0, cn):
        return ref.at[m, r0:r0 + rn, c0:c0 + cn]

    h = rows - side
    first, rest = (0, side, cols, side), (side, h, cols, side)
    under, corner = (rows, side, 0, cols), (rows, side, cols, side)
    hops = [
        (piece(obj, 0, side, 0, side), first, v > 0, right, left_dev),
        (piece(obj, 0, side, 0, cols), under, u > 0, below, up_dev),
        (piece(obj, side, h, 0, side), rest, v > 0, right, left_dev),
        (piece(ext, *first), corner, (u > 0) & right, below & right, up_dev),
    ]
    outs, fwds = [], []
    for n, (src, place, goes, comes, target) in enumerate(hops):
        outs.append(remote(src, piece(ext, *place), send.at[n], recv.at[n], target))
        fwds.append(remote(piece(ext, *place), piece(ext, *place), send.at[4 + n], recv.at[4 + n], other))
    for n in range(3):
        @pl.when(hops[n][2])
        def _(n=n):
            outs[n].start()
    mine = pl.ds(m * pm, pm)
    pc = remote(probe, full.at[:, mine], send.at[8], recv.at[8], other)
    pc.start()
    ext[:, 0:rows, 0:cols] = obj[...]
    full[:, mine] = probe[...]
    for n, (src, place, goes, comes, target) in enumerate(hops):
        @pl.when(comes)
        def _(n=n):
            outs[n].wait_recv()
            if n == 0:
                @pl.when(u > 0)
                def _():
                    outs[3].start()
            fwds[n].start()
    for n, (src, place, goes, comes, target) in enumerate(hops):
        @pl.when(goes)
        def _(n=n):
            outs[n].wait_send()

        @pl.when(comes)
        def _(n=n):
            fwds[n].wait()
    pc.wait()


def reduce_kernel(nx, ny, grad, pg, out, pout, rt_r, rt_l, rl, rp, low, edge, r_r, r_b, r_d,
                  acc, rx, px, ry, py, send, recv):
    u, v, m = lax.axis_index("gx"), lax.axis_index("gy"), lax.axis_index("ma")
    side = pg.shape[2]
    rows, cols = out.shape[1], out.shape[2]
    total = rows * 2
    pm = pg.shape[1] // 2
    o = 1 - m
    other = (u, v, o)
    last_x, last_y = nx - 1, ny - 1
    barrier = pltpu.get_barrier_semaphore()
    greet(barrier, other)
    for d in range(1, nx):
        greet(barrier, (lax.rem(u + d, nx), v, m))
        greet(barrier, (lax.rem(u + d, nx), v, o))
    for d in range(1, ny):
        greet(barrier, (u, lax.rem(v + d, ny), m))
    peers = 2 * nx + ny - 2
    pl.semaphore_wait(barrier, peers)

    theirs = pl.ds(pl.multiple_of(o * rows, 8), rows)
    mine = pl.ds(pl.multiple_of(m * rows, 8), rows)
    swaps = [
        remote(pg.at[:, pl.ds(o * pm, pm)], rp, send.at[0], recv.at[0], other),
        remote(grad.at[o, total:total + side, :], rl, send.at[1], recv.at[1], other),
        remote(grad.at[:, theirs, cols:cols + side], rt_r, send.at[2], recv.at[2], other),
        remote(grad.at[:, theirs, 0:cols], rt_l, send.at[3], recv.at[3], other),
    ]
    for c in swaps:
        c.start()
    swaps[0].wait_recv()
    for a in range(2):
        for b in range(pm):
            at = (a * pm + b) * side
            acc[at:at + side, :] = pg[a, m * pm + b] + rp[a, b]
    big = acc.shape[0] // nx
    small = big // ny
    gx_rs = []
    for d in range(1, nx):
        to = lax.rem(u + d, nx)
        c = remote(acc.at[pl.ds(pl.multiple_of(to * big, 8), big)], rx.at[d - 1], send.at[7 + d], recv.at[7 + d],
                   (to, v, m))
        c.start()
        gx_rs.append(c)
    swaps[1].wait_recv()
    low[...] = grad[m, total:total + side, :] + rl[...]
    c_b = remote(low, r_b.at[m], send.at[4], recv.at[4 + m], (u + 1, v, 0))
    c_d = remote(r_b.at[:, :, cols:cols + side], r_d, send.at[5], recv.at[6], (u, v + 1, 0))
    c_r = remote(edge, r_r, send.at[6], recv.at[3 + 5 + 2 * nx], (u, v + 1, m))
    swaps[2].wait_recv()
    edge[...] = grad[:, mine, cols:cols + side] + rt_r[...]

    @pl.when(v < last_y)
    def _():
        c_r.start()
    for c in gx_rs:
        c.wait_recv()

    @pl.when(u < last_x)
    def _():
        c_b.start()
    px[...] = acc[pl.ds(pl.multiple_of(u * big, 8), big), :]
    for d in range(1, nx):
        px[...] += rx[d - 1]
    base = 9 + 2 * nx
    gy_rs = []
    for d in range(1, ny):
        to = lax.rem(v + d, ny)
        c = remote(px.at[pl.ds(pl.multiple_of(to * small, 8), small)], ry.at[d - 1], send.at[base + d],
                   recv.at[base + d], (u, to, m))
        c.start()
        gy_rs.append(c)
    swaps[3].wait_recv()
    out[...] = grad[:, mine, 0:cols] + rt_l[...]
    for c in gy_rs:
        c.wait_recv()
    here = pl.ds(pl.multiple_of(u * big + v * small, 8), small)
    part = px[pl.ds(pl.multiple_of(v * small, 8), small), :]
    for d in range(1, ny):
        part = part + ry[d - 1]
    py[...] = part
    pout[here, :] = part
    base = base + ny
    gy_ag = []
    for d in range(1, ny):
        to = lax.rem(v + d, ny)
        c = remote(py, pout.at[here], send.at[base + d], recv.at[base + d], (u, to, m))
        c.start()
        gy_ag.append(c)
    for c in gy_ag:
        c.wait_recv()
    band = pl.ds(pl.multiple_of(u * big, 8), big)
    gx_ag = []
    for d in range(1, nx):
        to = lax.rem(u + d, nx)
        c = remote(pout.at[band], pout.at[band], send.at[7 + nx + d], recv.at[7 + nx + d], (to, v, m))
        c.start()
        gx_ag.append(c)

    @pl.when(v > 0)
    def _():
        c_r.wait_recv()
        out[:, :, 0:side] += r_r[...]

    @pl.when((u > 0) & (m == 0))
    def _():
        for k in range(2):
            remote(low, r_b.at[k], send.at[4], recv.at[4 + k], other).wait_recv()

        @pl.when(v < last_y)
        def _():
            c_d.start()
        out[:, 0:side, :] += r_b[:, :, 0:cols]

        @pl.when(v > 0)
        def _():
            c_d.wait_recv()
            out[:, 0:side, 0:side] += r_d[...]
    for c in gx_ag:
        c.wait_recv()
    for c in swaps + gx_rs + gy_rs + gy_ag + gx_ag:
        c.wait_send()

    @pl.when(u < last_x)
    def _():
        c_b.wait_send()

    @pl.when((u > 0) & (v < last_y) & (m == 0))
    def _():
        c_d.wait_send()

    @pl.when(v < last_y)
    def _():
        c_r.wait_send()


def local(nx, ny, object_field, probe, offsets, counts, amplitude):
    side = probe.shape[2]
    own_modes = probe.shape[1]
    modes = own_modes * 2
    rows, cols = object_field.shape[1:]
    cap = offsets.shape[2]
    dma = pltpu.SemaphoreType.DMA
    ext, full = pl.pallas_call(
        functools.partial(halo_kernel, nx, ny),
        name="halo",
        out_shape=(jax.ShapeDtypeStruct((2, rows + side, cols + side), F32),
                   jax.ShapeDtypeStruct((2, modes, side, side), F32)),
        in_specs=[VM, VM],
        out_specs=(VM, VM),
        scratch_shapes=[dma((9,)), dma((9,))],
        cost_estimate=pl.CostEstimate(flops=0, transcendentals=0, bytes_accessed=64 << 20),
        compiler_params=pltpu.CompilerParams(collective_id=0, has_side_effects=True, vmem_limit_bytes=12 << 20),
    )(object_field, probe)
    tall, wide, picks = tables(side)
    core = lax.axis_index("ma").astype(jnp.int32).reshape(1)
    grad, pg = pl.pallas_call(
        solve_kernel,
        name="solve",
        out_shape=(jax.ShapeDtypeStruct(ext.shape, F32), jax.ShapeDtypeStruct(full.shape, F32)),
        in_specs=[SM, SM, SM] + [VM] * 6,
        out_specs=(VM, VM),
        scratch_shapes=[pltpu.VMEM((modes, side, side), F32), pltpu.VMEM((modes, side, side), F32)],
        compiler_params=pltpu.CompilerParams(vmem_limit_bytes=24 << 20),
    )(offsets[0, 0], counts[0], core, ext, full, amplitude[0, 0],
      jnp.asarray(tall), jnp.asarray(wide), jnp.asarray(picks))
    half = rows // 2
    flat = 2 * own_modes * side
    big = flat // nx
    nsem = 9 + 2 * nx + 2 * ny + 2
    object_grad, probe_grad = pl.pallas_call(
        functools.partial(reduce_kernel, nx, ny),
        name="reduce",
        out_shape=(jax.ShapeDtypeStruct((2, half, cols), F32), jax.ShapeDtypeStruct((flat, side), F32)),
        in_specs=[VM, VM],
        out_specs=(VM, VM),
        scratch_shapes=[
            pltpu.VMEM((2, half, side), F32), pltpu.VMEM((2, half, cols), F32),
            pltpu.VMEM((side, cols + side), F32), pltpu.VMEM((2, own_modes, side, side), F32),
            pltpu.VMEM((side, cols + side), F32), pltpu.VMEM((2, half, side), F32),
            pltpu.VMEM((2, half, side), F32), pltpu.VMEM((2, side, cols + side), F32), pltpu.VMEM((2, side, side), F32),
            pltpu.VMEM((flat, side), F32), pltpu.VMEM((nx - 1, big, side), F32), pltpu.VMEM((big, side), F32),
            pltpu.VMEM((ny - 1, big // ny, side), F32), pltpu.VMEM((big // ny, side), F32),
            dma((nsem,)), dma((nsem,)),
        ],
        compiler_params=pltpu.CompilerParams(collective_id=1, has_side_effects=True, vmem_limit_bytes=18 << 20),
    )(grad, pg)
    return object_grad, probe_grad.reshape(2, own_modes, side, side)


def solution(mesh):
    return jax.shard_map(
        functools.partial(local, mesh.shape["gx"], mesh.shape["gy"]),
        mesh=mesh,
        in_specs=(
            P(None, "gx", "gy"),
            P(None, "ma", None, None),
            P("gx", "gy", None, None),
            P("gx", "gy"),
            P("gx", "gy", None, None, None),
        ),
        out_specs=(P(None, ("gx", "ma"), "gy"), P(None, "ma", None, None)),
        check_vma=False,
    )
```

```python
import functools

import jax
import jax.numpy as jnp
import ml_dtypes
import numpy as np
from jax import lax
from jax.experimental import pallas as pl
from jax.experimental.pallas import tpu as pltpu
from jax.sharding import PartitionSpec as P

F32 = jnp.float32
BF16 = jnp.bfloat16
MESH = pl.DeviceIdType.MESH
ANY = pl.BlockSpec(memory_space=pltpu.HBM)
SM = pl.BlockSpec(memory_space=pltpu.SMEM)
VM = pl.BlockSpec(memory_space=pltpu.VMEM)


def tables(side):
    half = side // 2
    line = np.arange(half)
    found = []
    for odd in (0, 1):
        product = (2 * line[:, None] + odd) * line[None, :] % side
        value = np.exp(-2j * np.pi * product / side) / np.sqrt(side)
        block = np.block([[value.real, -value.imag], [value.imag, value.real]])
        found.append(block)

    def parts(block):
        high = block.astype(np.float32).astype(ml_dtypes.bfloat16)
        low = (block - high.astype(np.float64)).astype(np.float32).astype(ml_dtypes.bfloat16)
        return high, high, low

    tall = [np.concatenate(parts(b), 0) for b in (found[0].T, found[1].T, found[0], found[1])]
    wide = [np.concatenate(parts(b), 1) for b in (found[0], found[1], found[0].T, found[1].T)]
    order = np.concatenate([np.arange(0, side, 2), np.arange(1, side, 2)])
    pick = np.zeros((side, side), np.float32)
    pick[order, np.arange(side)] = 1.0
    picks = np.stack([pick, pick.T]).astype(ml_dtypes.bfloat16)
    return np.stack(tall), np.stack(wide), picks


def split(x):
    high = x.astype(BF16)
    return high, (x - high.astype(F32)).astype(BF16)


def right_mul(x, table):
    high, low = split(x)
    return jnp.dot(jnp.concatenate([high, low, high], 1), table, preferred_element_type=F32)


def left_mul(table, x):
    high, low = split(x)
    return jnp.dot(table, jnp.concatenate([high, low, high], 0), preferred_element_type=F32)


def solve_kernel(off_ref, cnt_ref, core_ref, ext_ref, probe_ref, amp_ref, tall_hbm, wide_hbm, pick_ref,
                 grad_ref, pg_ref, far_e, far_o, tall_ref, wide_ref, sem):
    modes, side = probe_ref.shape[1], probe_ref.shape[2]
    half = side // 2
    fetches = [pltpu.make_async_copy(tall_hbm, tall_ref, sem.at[0]),
               pltpu.make_async_copy(wide_hbm, wide_ref, sem.at[1])]
    for c in fetches:
        c.start()
    grad_ref[...] = jnp.zeros_like(grad_ref)
    pg_ref[...] = jnp.zeros_like(pg_ref)
    for c in fetches:
        c.wait()

    @pl.loop(0, (cnt_ref[0] + 1 - core_ref[0]) // 2)
    def _(step):
        slot = 2 * step + core_ref[0]
        row = off_ref[slot, 0]
        col = off_ref[slot, 1]
        base = pl.multiple_of(col // 128 * 128, 128)
        shift = col - base
        width = side + 128
        top_row = pl.multiple_of(row // 8 * 8, 8)
        drop = row - top_row
        tall = side + 8
        window = (pl.ds(top_row, tall), pl.ds(base, width))

        def take(part):
            wide = ext_ref[(part, *window)]
            wide = pltpu.roll(wide, lax.rem(width - shift, width), 1)[:, :side]
            return pltpu.roll(wide, lax.rem(tall - drop, tall), 0)[:side]

        a_re, a_im = take(0), take(1)
        pow_e = pow_o = jnp.zeros((half, side), F32)
        for m in range(modes):
            p_re, p_im = probe_ref[0, m], probe_ref[1, m]
            e_re = p_re * a_re - p_im * a_im
            e_im = p_re * a_im + p_im * a_re
            x_e = jnp.concatenate([e_re[:, :half] + e_re[:, half:], e_im[:, :half] + e_im[:, half:]], 1)
            x_o = jnp.concatenate([e_re[:, :half] - e_re[:, half:], e_im[:, :half] - e_im[:, half:]], 1)
            z_e = right_mul(x_e, tall_ref[0])
            z_o = right_mul(x_o, tall_ref[1])
            z_re = jnp.concatenate([z_e[:, :half], z_o[:, :half]], 1)
            z_im = jnp.concatenate([z_e[:, half:], z_o[:, half:]], 1)
            y_e = jnp.concatenate([z_re[:half] + z_re[half:], z_im[:half] + z_im[half:]], 0)
            y_o = jnp.concatenate([z_re[:half] - z_re[half:], z_im[:half] - z_im[half:]], 0)
            f_e = left_mul(wide_ref[0], y_e)
            f_o = left_mul(wide_ref[1], y_o)
            far_e[m] = f_e
            far_o[m] = f_o
            pow_e = pow_e + (f_e[:half] * f_e[:half] + f_e[half:] * f_e[half:])
            pow_o = pow_o + (f_o[:half] * f_o[:half] + f_o[half:] * f_o[half:])
        measured = jnp.zeros((side, side), F32)
        for term in split(amp_ref[slot]):
            moved = jnp.dot(term, pick_ref[0], preferred_element_type=F32).astype(BF16)
            measured = measured + jnp.dot(pick_ref[1], moved, preferred_element_type=F32)
        fac_e = 1.0 - measured[:half] * lax.rsqrt(jnp.maximum(pow_e, 0.25))
        fac_o = 1.0 - measured[half:] * lax.rsqrt(jnp.maximum(pow_o, 0.25))
        fac_e = jnp.concatenate([fac_e, fac_e], 0)
        fac_o = jnp.concatenate([fac_o, fac_o], 0)
        g_re = g_im = jnp.zeros((side, side), F32)
        for m in range(modes):
            q_e = left_mul(wide_ref[2], far_e[m] * fac_e)
            q_o = left_mul(wide_ref[3], far_o[m] * fac_o)
            top, low = q_e + q_o, q_e - q_o
            w_re = jnp.concatenate([top[:half], low[:half]], 0)
            w_im = jnp.concatenate([top[half:], low[half:]], 0)
            s_e = right_mul(jnp.concatenate([w_re[:, :half], w_im[:, :half]], 1), tall_ref[2])
            s_o = right_mul(jnp.concatenate([w_re[:, half:], w_im[:, half:]], 1), tall_ref[3])
            first, second = s_e + s_o, s_e - s_o
            b_re = jnp.concatenate([first[:, :half], second[:, :half]], 1)
            b_im = jnp.concatenate([first[:, half:], second[:, half:]], 1)
            pg_ref[0, m] += a_re * b_re + a_im * b_im
            pg_ref[1, m] += a_re * b_im - a_im * b_re
            p_re, p_im = probe_ref[0, m], probe_ref[1, m]
            g_re = g_re + (p_re * b_re + p_im * b_im)
            g_im = g_im + (p_re * b_im - p_im * b_re)
        for part, value in ((0, g_re), (1, g_im)):
            long = pltpu.roll(jnp.concatenate([value, jnp.zeros((8, side), F32)], 0), drop, 0)
            wide = jnp.concatenate([long, jnp.zeros((tall, 128), F32)], 1)
            grad_ref[(part, *window)] += pltpu.roll(wide, shift, 1)


def remote(src, dst, send, recv, where):
    return pltpu.make_async_remote_copy(src_ref=src, dst_ref=dst, send_sem=send, recv_sem=recv,
                                        device_id=where, device_id_type=MESH)


def greet(barrier, where):
    pl.semaphore_signal(barrier, inc=1, device_id=where, device_id_type=MESH)


def halo_kernel(nx, ny, obj, probe, ext, full, send, recv):
    u, v, m = lax.axis_index("gx"), lax.axis_index("gy"), lax.axis_index("ma")
    side = probe.shape[2]
    rows, cols = obj.shape[1], obj.shape[2]
    pm = probe.shape[1]
    other = (u, v, 1 - m)
    right, below = v < ny - 1, u < nx - 1
    left_dev, right_dev = (u, v - 1, m), (u, v + 1, m)
    up_dev, down_dev = (u - 1, v, m), (u + 1, v, m)
    barrier = pltpu.get_barrier_semaphore()
    greet(barrier, other)
    peers = 1
    for there, where in ((v > 0, left_dev), (right, right_dev), (u > 0, up_dev), (below, down_dev)):
        peers = peers + jnp.where(there, 1, 0)

        @pl.when(there)
        def _(where=where):
            greet(barrier, where)
    pl.semaphore_wait(barrier, peers)

    def piece(ref, r0, rn, c0, cn):
        return ref.at[m, r0:r0 + rn, c0:c0 + cn]

    h = rows - side
    first, rest = (0, side, cols, side), (side, h, cols, side)
    under, corner = (rows, side, 0, cols), (rows, side, cols, side)
    hops = [
        (piece(obj, 0, side, 0, side), first, v > 0, right, left_dev),
        (piece(obj, 0, side, 0, cols), under, u > 0, below, up_dev),
        (piece(obj, side, h, 0, side), rest, v > 0, right, left_dev),
        (piece(ext, *first), corner, (u > 0) & right, below & right, up_dev),
    ]
    outs, fwds = [], []
    for n, (src, place, goes, comes, target) in enumerate(hops):
        outs.append(remote(src, piece(ext, *place), send.at[n], recv.at[n], target))
        fwds.append(remote(piece(ext, *place), piece(ext, *place), send.at[4 + n], recv.at[4 + n], other))
    for n in range(3):
        @pl.when(hops[n][2])
        def _(n=n):
            outs[n].start()
    mine = pl.ds(m * pm, pm)
    pc = remote(probe, full.at[:, mine], send.at[8], recv.at[8], other)
    pc.start()
    ext[:, 0:rows, 0:cols] = obj[...]
    full[:, mine] = probe[...]
    for n, (src, place, goes, comes, target) in enumerate(hops):
        @pl.when(comes)
        def _(n=n):
            outs[n].wait_recv()
            if n == 0:
                @pl.when(u > 0)
                def _():
                    outs[3].start()
            fwds[n].start()
    for n, (src, place, goes, comes, target) in enumerate(hops):
        @pl.when(goes)
        def _(n=n):
            outs[n].wait_send()

        @pl.when(comes)
        def _(n=n):
            fwds[n].wait()
    pc.wait()


def reduce_kernel(nx, ny, grad, pg, out, pout, rt_r, rt_l, rl, rp, low, edge, r_r, r_b, r_d,
                  acc, rx, px, ry, py, send, recv):
    u, v, m = lax.axis_index("gx"), lax.axis_index("gy"), lax.axis_index("ma")
    side = pg.shape[2]
    rows, cols = out.shape[1], out.shape[2]
    total = rows * 2
    pm = pg.shape[1] // 2
    o = 1 - m
    other = (u, v, o)
    last_x, last_y = nx - 1, ny - 1
    barrier = pltpu.get_barrier_semaphore()
    greet(barrier, other)
    for d in range(1, nx):
        greet(barrier, (lax.rem(u + d, nx), v, m))
        greet(barrier, (lax.rem(u + d, nx), v, o))
    for d in range(1, ny):
        greet(barrier, (u, lax.rem(v + d, ny), m))
    peers = 2 * nx + ny - 2
    pl.semaphore_wait(barrier, peers)

    theirs = pl.ds(pl.multiple_of(o * rows, 8), rows)
    mine = pl.ds(pl.multiple_of(m * rows, 8), rows)
    swaps = [
        remote(pg.at[:, pl.ds(o * pm, pm)], rp, send.at[0], recv.at[0], other),
        remote(grad.at[o, total:total + side, :], rl, send.at[1], recv.at[1], other),
        remote(grad.at[:, theirs, cols:cols + side], rt_r, send.at[2], recv.at[2], other),
        remote(grad.at[:, theirs, 0:cols], rt_l, send.at[3], recv.at[3], other),
    ]
    for c in swaps:
        c.start()
    swaps[0].wait_recv()
    for a in range(2):
        for b in range(pm):
            at = (a * pm + b) * side
            acc[at:at + side, :] = pg[a, m * pm + b] + rp[a, b]
    big = acc.shape[0] // nx
    small = big // ny
    gx_rs = []
    for d in range(1, nx):
        to = lax.rem(u + d, nx)
        c = remote(acc.at[pl.ds(pl.multiple_of(to * big, 8), big)], rx.at[d - 1], send.at[7 + d], recv.at[7 + d],
                   (to, v, m))
        c.start()
        gx_rs.append(c)
    swaps[1].wait_recv()
    low[...] = grad[m, total:total + side, :] + rl[...]
    c_b = remote(low, r_b.at[m], send.at[4], recv.at[4 + m], (u + 1, v, 0))
    c_d = remote(r_b.at[:, :, cols:cols + side], r_d, send.at[5], recv.at[6], (u, v + 1, 0))
    c_r = remote(edge, r_r, send.at[6], recv.at[3 + 5 + 2 * nx], (u, v + 1, m))
    swaps[2].wait_recv()
    edge[...] = grad[:, mine, cols:cols + side] + rt_r[...]

    @pl.when(v < last_y)
    def _():
        c_r.start()
    for c in gx_rs:
        c.wait_recv()

    @pl.when(u < last_x)
    def _():
        c_b.start()
    px[...] = acc[pl.ds(pl.multiple_of(u * big, 8), big), :]
    for d in range(1, nx):
        px[...] += rx[d - 1]
    base = 9 + 2 * nx
    gy_rs = []
    for d in range(1, ny):
        to = lax.rem(v + d, ny)
        c = remote(px.at[pl.ds(pl.multiple_of(to * small, 8), small)], ry.at[d - 1], send.at[base + d],
                   recv.at[base + d], (u, to, m))
        c.start()
        gy_rs.append(c)
    swaps[3].wait_recv()
    out[...] = grad[:, mine, 0:cols] + rt_l[...]
    for c in gy_rs:
        c.wait_recv()
    here = pl.ds(pl.multiple_of(u * big + v * small, 8), small)
    part = px[pl.ds(pl.multiple_of(v * small, 8), small), :]
    for d in range(1, ny):
        part = part + ry[d - 1]
    py[...] = part
    pout[here, :] = part
    base = base + ny
    gy_ag = []
    for d in range(1, ny):
        to = lax.rem(v + d, ny)
        c = remote(py, pout.at[here], send.at[base + d], recv.at[base + d], (u, to, m))
        c.start()
        gy_ag.append(c)
    for c in gy_ag:
        c.wait_recv()
    band = pl.ds(pl.multiple_of(u * big, 8), big)
    gx_ag = []
    for d in range(1, nx):
        to = lax.rem(u + d, nx)
        c = remote(pout.at[band], pout.at[band], send.at[7 + nx + d], recv.at[7 + nx + d], (to, v, m))
        c.start()
        gx_ag.append(c)

    @pl.when(v > 0)
    def _():
        c_r.wait_recv()
        out[:, :, 0:side] += r_r[...]

    @pl.when((u > 0) & (m == 0))
    def _():
        for k in range(2):
            remote(low, r_b.at[k], send.at[4], recv.at[4 + k], other).wait_recv()

        @pl.when(v < last_y)
        def _():
            c_d.start()
        out[:, 0:side, :] += r_b[:, :, 0:cols]

        @pl.when(v > 0)
        def _():
            c_d.wait_recv()
            out[:, 0:side, 0:side] += r_d[...]
    for c in gx_ag:
        c.wait_recv()
    for c in swaps + gx_rs + gy_rs + gy_ag + gx_ag:
        c.wait_send()

    @pl.when(u < last_x)
    def _():
        c_b.wait_send()

    @pl.when((u > 0) & (v < last_y) & (m == 0))
    def _():
        c_d.wait_send()

    @pl.when(v < last_y)
    def _():
        c_r.wait_send()


def local(nx, ny, object_field, probe, offsets, counts, amplitude):
    side = probe.shape[2]
    own_modes = probe.shape[1]
    modes = own_modes * 2
    rows, cols = object_field.shape[1:]
    cap = offsets.shape[2]
    dma = pltpu.SemaphoreType.DMA
    ext, full = pl.pallas_call(
        functools.partial(halo_kernel, nx, ny),
        name="halo",
        out_shape=(jax.ShapeDtypeStruct((2, rows + side, cols + side), F32),
                   jax.ShapeDtypeStruct((2, modes, side, side), F32)),
        in_specs=[VM, VM],
        out_specs=(VM, VM),
        scratch_shapes=[dma((9,)), dma((9,))],
        cost_estimate=pl.CostEstimate(flops=0, transcendentals=0, bytes_accessed=64 << 20),
        compiler_params=pltpu.CompilerParams(collective_id=0, has_side_effects=True, vmem_limit_bytes=12 << 20),
    )(object_field, probe)
    tall, wide, picks = tables(side)
    core = lax.axis_index("ma").astype(jnp.int32).reshape(1)
    grad, pg = pl.pallas_call(
        solve_kernel,
        name="solve",
        out_shape=(jax.ShapeDtypeStruct(ext.shape, F32), jax.ShapeDtypeStruct(full.shape, F32)),
        in_specs=[SM, SM, SM, VM, VM, VM, ANY, ANY, VM],
        out_specs=(VM, VM),
        scratch_shapes=[pltpu.VMEM((modes, side, side), F32), pltpu.VMEM((modes, side, side), F32),
                        pltpu.VMEM(tall.shape, BF16), pltpu.VMEM(wide.shape, BF16), dma((2,))],
        compiler_params=pltpu.CompilerParams(vmem_limit_bytes=24 << 20),
    )(offsets[0, 0], counts[0], core, ext, full, amplitude[0, 0],
      jnp.asarray(tall), jnp.asarray(wide), jnp.asarray(picks))
    half = rows // 2
    flat = 2 * own_modes * side
    big = flat // nx
    nsem = 9 + 2 * nx + 2 * ny + 2
    object_grad, probe_grad = pl.pallas_call(
        functools.partial(reduce_kernel, nx, ny),
        name="reduce",
        out_shape=(jax.ShapeDtypeStruct((2, half, cols), F32), jax.ShapeDtypeStruct((flat, side), F32)),
        in_specs=[VM, VM],
        out_specs=(VM, VM),
        scratch_shapes=[
            pltpu.VMEM((2, half, side), F32), pltpu.VMEM((2, half, cols), F32),
            pltpu.VMEM((side, cols + side), F32), pltpu.VMEM((2, own_modes, side, side), F32),
            pltpu.VMEM((side, cols + side), F32), pltpu.VMEM((2, half, side), F32),
            pltpu.VMEM((2, half, side), F32), pltpu.VMEM((2, side, cols + side), F32), pltpu.VMEM((2, side, side), F32),
            pltpu.VMEM((flat, side), F32), pltpu.VMEM((nx - 1, big, side), F32), pltpu.VMEM((big, side), F32),
            pltpu.VMEM((ny - 1, big // ny, side), F32), pltpu.VMEM((big // ny, side), F32),
            dma((nsem,)), dma((nsem,)),
        ],
        compiler_params=pltpu.CompilerParams(collective_id=1, has_side_effects=True, vmem_limit_bytes=18 << 20),
    )(grad, pg)
    return object_grad, probe_grad.reshape(2, own_modes, side, side)


def solution(mesh):
    return jax.shard_map(
        functools.partial(local, mesh.shape["gx"], mesh.shape["gy"]),
        mesh=mesh,
        in_specs=(
            P(None, "gx", "gy"),
            P(None, "ma", None, None),
            P("gx", "gy", None, None),
            P("gx", "gy"),
            P("gx", "gy", None, None, None),
        ),
        out_specs=(P(None, ("gx", "ma"), "gy"), P(None, "ma", None, None)),
        check_vma=False,
    )
```
